32 devices in a mesh: pipe: 8 (over z, y), dp: 4 (over x, core).
Axes of the slice: x: 2, y: 2, z: 4, core: 2. Of those that a mesh axis runs over, the one named last changes fastest.
Arguments:
- grad_output: bfloat16 [512, 8192], P('dp'), may hold values from -6 to 6
- hidden: bfloat16 [512, 14336], P('dp', 'pipe'), may hold values from -6 to 6
- next_hidden: bfloat16 [512, 14336], P('dp', 'pipe'), may hold values from -6 to 6
- master: float32 [14336, 8192], P('pipe', 'dp'), may hold values from -0.046875 to 0.046875
- moment: float32 [14336, 8192], P('pipe', 'dp'), may hold values from -24 to 24
- second_moment: float32 [14336, 8192], P('pipe', 'dp'), may hold values from 5 to 100
Outputs:
- update: float32 [14336, 8192], P('pipe', 'dp')
- upstream_grad: bfloat16 [512, 14336], P('dp', 'pipe')
- next_output: bfloat16 [512, 8192], P('pipe', 'dp')
The draws below stay inside these ranges and needn't reach their ends.
All inputs are finite; a program needn't handle non-finite values.
Results may differ from the reference program's by a relative error of at most 0.005.
Values may be sent and summed in bfloat16 or wider, within the bound.
A program may use at most 256 MiB of HBM per device.

```python
import math
import jax
import jax.numpy as jnp
from jax import lax

D = 8192
FF = 14336
TOKENS = 512


def levels(key, dims, cuts, low, high):
    level = 1.0
    for dim, shards_of in cuts:
        steps = jax.random.uniform(jax.random.fold_in(jax.random.fold_in(key, 6), dim), (shards_of,), jnp.float32, low / len(cuts), high / len(cuts))
        level = level * jnp.repeat(jnp.exp(steps), dims[dim] // shards_of).reshape((-1,) + (1,) * (len(dims) - 1 - dim))
    return level


def bell_draw(key, shape, width, limit, split=(), dtype=jnp.bfloat16):
    level = levels(key, shape, split, -0.22, 0.18) if split else 1.0
    result = jax.random.normal(key, shape, jnp.float32) * width * level
    return jnp.minimum(jnp.maximum(result, -limit), limit).astype(dtype)


def setup_inputs(seed: int = 0) -> dict:
    key_list = jax.random.split(jax.random.key(seed), 7)
    grad_output = bell_draw(key_list[0], (TOKENS, D), 1.0, 6.0, ((0, 4),))
    hidden = bell_draw(key_list[1], (TOKENS, FF), 1.0, 6.0, ((0, 4), (1, 8)))
    next_hidden = bell_draw(key_list[2], (TOKENS, FF), 1.0, 6.0, ((0, 4), (1, 8)))
    master = bell_draw(key_list[3], (FF, D), FF ** -0.5, 0.046875, ((0, 8), (1, 4)), jnp.float32)
    moment = bell_draw(key_list[4], (FF, D), 4.0, 24.0, ((0, 8), (1, 4)), jnp.float32)
    second_moment = jnp.clip(jnp.exp(math.log(100.0) - 2.9957323 * jax.random.uniform(key_list[5], (FF, D), jnp.float32) ** levels(key_list[5], (FF, D), ((0, 8), (1, 4)), -0.2, 0.2)), 5.0, 100.0)
    return {"grad_output": grad_output, "hidden": hidden, "next_hidden": next_hidden, "master": master, "moment": moment, "second_moment": second_moment}


beta_one = 0.9
beta_two = 0.95
corr_one = 1.0 - 0.9 ** 10
corr_two = 1.0 - 0.95 ** 10
learn_rate = 0.005
decay_rate = 0.1
epsilon = 1e-08

def reference(grad_output, hidden, next_hidden, master, moment, second_moment):
    weights_low = master.astype(jnp.bfloat16)
    upstream_grad = lax.dot_general(grad_output, weights_low, (((1,), (1,)), ((), ())), preferred_element_type=jnp.float32).astype(jnp.bfloat16)
    gradient = lax.dot_general(hidden, grad_output, (((0,), (0,)), ((), ())), preferred_element_type=jnp.float32)
    moment_new = beta_one * moment + (1.0 - beta_one) * gradient
    second_new = beta_two * second_moment + (1.0 - beta_two) * gradient * gradient
    update = -(moment_new / corr_one / (jnp.sqrt(second_new / corr_two) + epsilon) + decay_rate * master)
    fresh_low = (master + learn_rate * update).astype(jnp.bfloat16)
    next_output = jnp.dot(next_hidden, fresh_low, preferred_element_type=jnp.float32).astype(jnp.bfloat16)
    return (update, upstream_grad, next_output)
```

```python
import functools
import math

import jax
import jax.numpy as jnp
from jax import lax
from jax.experimental import pallas as pl
from jax.experimental.pallas import tpu as pltpu
from jax.sharding import PartitionSpec as P

beta_one = 0.9
beta_two = 0.95
corr_one = 1.0 - 0.9**10
corr_two = 1.0 - 0.95**10
learn_rate = 0.005
decay_rate = 0.1
epsilon = 1e-08

f32 = jnp.float32
bf16 = jnp.bfloat16
MESH = pl.DeviceIdType.MESH
ALL = slice(None)


def remote(src, dst, send, recv, pipe, dp):
    return pltpu.make_async_remote_copy(
        src_ref=src, dst_ref=dst, send_sem=send, recv_sem=recv,
        device_id=(pipe, dp), device_id_type=MESH,
    )


def greet(partners):
    barrier = pltpu.get_barrier_semaphore()
    for partner in partners:
        pl.semaphore_signal(barrier, inc=1, device_id=partner, device_id_type=MESH)
    pl.semaphore_wait(barrier, len(partners))


def gather_kernel(n_dp, share, g, hid, nxt, cols, h, nh, loc, sib_s, sib_r,
                  g_s, g_r, gf_s, gf_r, h_s, h_r, hf_s, hf_r):
    pipe, dp = lax.axis_index("pipe"), lax.axis_index("dp")
    chips = n_dp // 2
    chip, core = dp // 2, dp % 2
    sib = chip * 2 + 1 - core
    rows, width = cols.shape[1], cols.shape[2]
    part = rows // share
    q = pipe % share
    base = pipe - q
    mine = pl.ds(pl.multiple_of(q * part, part), part)

    def columns(d):
        return pl.ds(pl.multiple_of(d * width, width), width)

    mates = [base + (q + f) % share for f in range(1, share)]
    ahead = [(chip + o) % chips for o in range(chips)]
    behind = [(chip + chips - o) % chips for o in range(chips)]
    partners = [(pipe, sib)]
    partners += [(pipe, ahead[o] * 2 + (core + e) % 2) for o in range(1, chips) for e in range(2)]
    partners += [(m, dp) for m in mates]

    local = [
        pltpu.make_async_copy(g.at[:, columns(dp)], cols.at[dp], loc.at[0]),
        pltpu.make_async_copy(hid, h.at[dp], loc.at[1]),
        pltpu.make_async_copy(nxt, nh.at[dp], loc.at[2]),
    ]
    for c in local:
        c.start()
    greet(partners)

    pairs = ((hid, h), (nxt, nh))
    cross = {}
    for o in range(1, chips):
        for e in range(2):
            d = ahead[o] * 2 + (core + e) % 2
            cross[o, e] = remote(g.at[mine, columns(d)], cols.at[dp, mine],
                                 g_s.at[o, e], g_r.at[o, e], pipe, d)
            cross[o, e].start()
    hops = {}
    for i, (src, dst) in enumerate(pairs):
        for o in range(1, chips):
            hops[i, o] = remote(src, dst.at[dp], h_s.at[i, o], h_r.at[i, o],
                                pipe, ahead[o] * 2 + core)
            hops[i, o].start()
    side = [remote(g.at[:, columns(sib)], cols.at[dp], sib_s.at[0], sib_r.at[0], pipe, sib)]
    for i, (src, dst) in enumerate(pairs):
        side.append(remote(src, dst.at[dp], sib_s.at[i + 1], sib_r.at[i + 1], pipe, sib))
    for c in side:
        c.start()
    passed = []
    for o in range(1, chips):
        for e in range(2):
            cross[o, e].wait_recv()
            block = cols.at[behind[o] * 2 + (core + e) % 2, mine]
            for f, m in enumerate(mates):
                c = remote(block, block, gf_s.at[o, e, f], gf_r.at[o, e, f], m, dp)
                c.start()
                passed.append(c)
    for i, (src, dst) in enumerate(pairs):
        for o in range(1, chips):
            hops[i, o].wait_recv()
            block = dst.at[behind[o] * 2 + core]
            c = remote(block, block, hf_s.at[i, o], hf_r.at[i, o], pipe, sib)
            c.start()
            passed.append(c)
    for c in local:
        c.wait()
    for c in list(cross.values()) + list(hops.values()):
        c.wait_send()
    for c in side + passed:
        c.wait()


def gather(n_pipe, n_dp, g, hid, nxt):
    rows, ff = hid.shape
    width = g.shape[1] // n_dp
    chips = n_dp // 2
    share = 4 if n_pipe % 4 == 0 else 1
    anywhere = pl.BlockSpec(memory_space=pl.ANY)
    dma = pltpu.SemaphoreType.DMA
    mates = max(share - 1, 1)
    outs = pl.pallas_call(
        functools.partial(gather_kernel, n_dp, share),
        out_shape=[jax.ShapeDtypeStruct((n_dp, rows, w), bf16) for w in (width, ff, ff)],
        in_specs=[anywhere] * 3,
        out_specs=[anywhere] * 3,
        scratch_shapes=[
            dma((3,)), dma((3,)), dma((3,)),
            dma((chips, 2)), dma((chips, 2)),
            dma((chips, 2, mates)), dma((chips, 2, mates)),
            dma((2, chips)), dma((2, chips)), dma((2, chips)), dma((2, chips)),
        ],
        compiler_params=pltpu.CompilerParams(collective_id=1, has_side_effects=True),
        name="gather_all",
    )(g, hid, nxt)
    return [o.reshape(n_dp * rows, o.shape[2]) for o in outs]


def step_kernel(chunk, g_ref, h_ref, nh_ref, w_ref, m_ref, s_ref,
                up_ref, next_ref, update_ref, turned, total, fresh):
    j = pl.program_id(0)
    ff = h_ref.shape[1]

    @pl.when(j == 0)
    def _():
        total[...] = jnp.zeros_like(total)
        for c in range(0, ff, chunk):
            turned[pl.ds(c, chunk), :] = h_ref[:, pl.ds(c, chunk)].T

    for c in range(0, ff, chunk):
        r = pl.ds(c, chunk)
        grad = jnp.dot(turned[r, :], g_ref[...], preferred_element_type=f32)
        w = w_ref[r, :]
        total[:, r] += lax.dot_general(
            g_ref[...], w.astype(bf16), (((1,), (1,)), ((), ())), preferred_element_type=f32
        )
        top = (beta_one / corr_one) * m_ref[r, :] + ((1.0 - beta_one) / corr_one) * grad
        var = (beta_two / corr_two) * s_ref[r, :] + ((1.0 - beta_two) / corr_two) * (grad * grad)
        update = -(top / (var * lax.rsqrt(var) + epsilon) + decay_rate * w)
        update_ref[r, :] = update
        fresh[r, :] = (w + learn_rate * update).astype(bf16)
    next_ref[...] = jnp.dot(nh_ref[...], fresh[...], preferred_element_type=f32).astype(bf16)

    @pl.when(j == pl.num_programs(0) - 1)
    def _():
        up_ref[...] = total[...].astype(bf16)


def step(cols, h, nh, master, moment, second):
    tokens, width = cols.shape
    ff = h.shape[1]
    bn = 256 if width % 256 == 0 else width
    chunk = 256 if ff % 256 == 0 else 128
    whole = pl.BlockSpec((tokens, ff), lambda j: (0, 0), pipeline_mode=pl.Buffered(1))
    tall = pl.BlockSpec((ff, bn), lambda j: (0, j))
    slab = pl.BlockSpec((tokens, bn), lambda j: (0, j))
    return pl.pallas_call(
        functools.partial(step_kernel, chunk),
        grid=(width // bn,),
        out_shape=[
            jax.ShapeDtypeStruct((tokens, ff), bf16),
            jax.ShapeDtypeStruct((tokens, width), bf16),
            jax.ShapeDtypeStruct((ff, width), f32),
        ],
        in_specs=[slab, whole, whole, tall, tall, tall],
        out_specs=[pl.BlockSpec((tokens, ff), lambda j: (0, 0)), slab, tall],
        scratch_shapes=[
            pltpu.VMEM((ff, tokens), bf16),
            pltpu.VMEM((tokens, ff), f32),
            pltpu.VMEM((ff, bn), bf16),
        ],
        cost_estimate=pl.CostEstimate(
            flops=6 * tokens * ff * width, bytes_accessed=16 * ff * width, transcendentals=ff * width
        ),
        compiler_params=pltpu.CompilerParams(vmem_limit_bytes=56 << 20),
        name="fused_step",
    )(cols, h, nh, master, moment, second)


def reduce_kernel(levels, n_dp, pieces, up, nxt, up_out, next_out, *scratch):
    up_in, up_mid, up_far, us_s, us_r, uf_s, uf_r, n_s, n_r = scratch[:9]
    recv = scratch[9:9 + levels]
    send = (None,) + scratch[9 + levels:8 + 2 * levels]
    keep = (None,) + scratch[8 + 2 * levels:]
    pipe, dp = lax.axis_index("pipe"), lax.axis_index("dp")
    chips = n_dp // 2
    chip, core = dp // 2, dp % 2
    sib = chip * 2 + 1 - core
    ahead = [(chip + o) % chips for o in range(chips)]
    bit = [(pipe // 2**b) % 2 for b in range(levels)]
    across = [pipe + (1 - 2 * bit[b]) * 2**b for b in range(levels)]
    greet([(pipe, sib)] + [(pipe, ahead[o] * 2 + core) for o in range(1, chips)]
          + [(across[b], dp) for b in range(levels)])

    cw = next_out.shape[1] // pieces
    orders = []
    for k in range(pieces):
        order = list(range(levels))
        if k % 2 and levels > 1:
            order[0], order[1] = order[1], order[0]
        orders.append(order)

    def pick(k, j, value):
        left = sorted(orders[k][j:], reverse=True)
        at = left.index(orders[k][j])
        return (ALL,) * at + (value,) + (ALL,) * (len(left) - 1 - at)

    def spot(j, k):
        return (ALL,) * (levels - 1 - j) + (ALL, pl.ds(k * cw, cw))

    flights = {}

    def launch(j, k, src):
        b = orders[k][j]
        flights[j, k] = remote(src, recv[j].at[spot(j, k)], n_s.at[j, k], n_r.at[j, k], across[b], dp)
        flights[j, k].start()

    tail = lambda k: (ALL, pl.ds(k * cw, cw))
    for k in range(pieces):
        launch(0, k, nxt.at[pick(k, 0, 1 - bit[orders[k][0]]) + tail(k)])
    near = {}
    for o in list(range(1, chips)) + [0]:
        near[o] = remote(up.at[ahead[o], 1 - core], up_in.at[o], us_s.at[o], us_r.at[o], pipe, sib)
        near[o].start()
    far = {}
    for o in range(1, chips):
        near[o].wait_recv()
        up_mid[o] = (up[ahead[o], core].astype(f32) + up_in[o].astype(f32)).astype(bf16)
        far[o] = remote(up_mid.at[o], up_far.at[o], uf_s.at[o], uf_r.at[o], pipe, ahead[o] * 2 + core)
        far[o].start()

    for j in range(levels):
        for k in range(pieces):
            flights[j, k].wait_recv()

            def summed(index):
                if j == 0:
                    mine = pick(k, 0, bit[orders[k][0]])
                    full, i = [], iter(index)
                    for m in mine:
                        full.append(next(i) if isinstance(m, slice) else m)
                    kept = nxt[tuple(full) + tail(k)]
                else:
                    kept = keep[j][index + tail(k)]
                return kept.astype(f32) + recv[j][index + tail(k)].astype(f32)

            if j < levels - 1:
                b = bit[orders[k][j + 1]]
                send[j + 1][spot(j + 1, k)] = summed(pick(k, j + 1, 1 - b)).astype(bf16)
                launch(j + 1, k, send[j + 1].at[spot(j + 1, k)])
                keep[j + 1][spot(j + 1, k)] = summed(pick(k, j + 1, b))
            else:
                next_out[tail(k)] = summed(()).astype(bf16)

    near[0].wait_recv()
    total = up[chip, core].astype(f32) + up_in[0].astype(f32)
    for o in range(1, chips):
        far[o].wait_recv()
        total = total + up_far[o].astype(f32)
    up_out[...] = total.astype(bf16)
    for c in list(near.values()) + list(far.values()) + list(flights.values()):
        c.wait_send()


def reduce(n_pipe, n_dp, up, nxt):
    levels = int(math.log2(n_pipe))
    tokens, ff = up.shape
    width = nxt.shape[1]
    rows, few = tokens // n_dp, tokens // n_pipe
    chips = n_dp // 2
    pieces = 4 if width % 512 == 0 else 1
    dma = pltpu.SemaphoreType.DMA
    vmem = pl.BlockSpec(memory_space=pltpu.VMEM)
    shape = lambda j: (2,) * (levels - 1 - j) + (few, width)
    return pl.pallas_call(
        functools.partial(reduce_kernel, levels, n_dp, pieces),
        out_shape=[
            jax.ShapeDtypeStruct((rows, ff), bf16),
            jax.ShapeDtypeStruct((few, width), bf16),
        ],
        in_specs=[vmem] * 2,
        out_specs=[vmem] * 2,
        scratch_shapes=[pltpu.VMEM((chips, rows, ff), bf16)] * 3
        + [dma((chips,))] * 4
        + [dma((levels, pieces))] * 2
        + [pltpu.VMEM(shape(j), bf16) for j in range(levels)]
        + [pltpu.VMEM(shape(j), bf16) for j in range(1, levels)]
        + [pltpu.VMEM(shape(j), f32) for j in range(1, levels)],
        compiler_params=pltpu.CompilerParams(
            collective_id=2, has_side_effects=True, vmem_limit_bytes=48 << 20
        ),
        name="reduce_both",
    )(up.reshape(chips, 2, rows, ff), nxt.reshape((2,) * levels + (few, width)))


def on_device(n_pipe, n_dp, grad_output, hidden, next_hidden, master, moment, second_moment):
    cols, h, nh = gather(n_pipe, n_dp, grad_output, hidden, next_hidden)
    up, nxt, update = step(cols, h, nh, master, moment, second_moment)
    upstream, next_out = reduce(n_pipe, n_dp, up, nxt)
    return (update, upstream, next_out)


def solution(mesh):
    in_specs = (
        P("dp", None),
        P("dp", "pipe"),
        P("dp", "pipe"),
        P("pipe", "dp"),
        P("pipe", "dp"),
        P("pipe", "dp"),
    )
    out_specs = (P("pipe", "dp"), P("dp", "pipe"), P("pipe", "dp"))
    return jax.shard_map(
        functools.partial(on_device, mesh.shape["pipe"], mesh.shape["dp"]),
        mesh=mesh, in_specs=in_specs, out_specs=out_specs, check_vma=False,
    )
```

```python
import functools
import math

import jax
import jax.numpy as jnp
from jax import lax
from jax.experimental import pallas as pl
from jax.experimental.pallas import tpu as pltpu
from jax.sharding import PartitionSpec as P

beta_one = 0.9
beta_two = 0.95
corr_one = 1.0 - 0.9**10
corr_two = 1.0 - 0.95**10
learn_rate = 0.005
decay_rate = 0.1
epsilon = 1e-08

f32 = jnp.float32
bf16 = jnp.bfloat16
MESH = pl.DeviceIdType.MESH
ALL = slice(None)


def remote(src, dst, send, recv, pipe, dp):
    return pltpu.make_async_remote_copy(
        src_ref=src, dst_ref=dst, send_sem=send, recv_sem=recv,
        device_id=(pipe, dp), device_id_type=MESH,
    )


def greet(partners):
    barrier = pltpu.get_barrier_semaphore()
    for partner in partners:
        pl.semaphore_signal(barrier, inc=1, device_id=partner, device_id_type=MESH)
    pl.semaphore_wait(barrier, len(partners))


def gather_kernel(n_dp, share, g, hid, cols, h, loc, sib_s, sib_r,
                  g_s, g_r, gf_s, gf_r, h_s, h_r, hf_s, hf_r):
    pipe, dp = lax.axis_index("pipe"), lax.axis_index("dp")
    chips = n_dp // 2
    chip, core = dp // 2, dp % 2
    sib = chip * 2 + 1 - core
    rows, width = cols.shape[1], cols.shape[2]
    part = rows // share
    q = pipe % share
    base = pipe - q
    mine = pl.ds(pl.multiple_of(q * part, part), part)

    def columns(d):
        return pl.ds(pl.multiple_of(d * width, width), width)

    mates = [base + (q + f) % share for f in range(1, share)]
    ahead = [(chip + o) % chips for o in range(chips)]
    behind = [(chip + chips - o) % chips for o in range(chips)]
    partners = [(pipe, sib)]
    partners += [(pipe, ahead[o] * 2 + (core + e) % 2) for o in range(1, chips) for e in range(2)]
    partners += [(m, dp) for m in mates]

    local = [
        pltpu.make_async_copy(g.at[:, columns(dp)], cols.at[dp], loc.at[0]),
        pltpu.make_async_copy(hid, h.at[dp], loc.at[1]),
    ]
    for c in local:
        c.start()
    greet(partners)

    cross = {}
    for o in range(1, chips):
        for e in range(2):
            d = ahead[o] * 2 + (core + e) % 2
            cross[o, e] = remote(g.at[mine, columns(d)], cols.at[dp, mine],
                                 g_s.at[o, e], g_r.at[o, e], pipe, d)
            cross[o, e].start()
    half = rows // 2
    hops = {}
    for o in range(1, chips):
        for i in range(2):
            some = pl.ds(i * half, half)
            hops[o, i] = remote(hid.at[some], h.at[dp, some], h_s.at[o, i], h_r.at[o, i],
                                pipe, ahead[o] * 2 + core)
            hops[o, i].start()
    side = [
        remote(g.at[:, columns(sib)], cols.at[dp], sib_s.at[0], sib_r.at[0], pipe, sib),
        remote(hid, h.at[dp], sib_s.at[1], sib_r.at[1], pipe, sib),
    ]
    for c in side:
        c.start()
    passed = []
    for o in range(1, chips):
        for e in range(2):
            cross[o, e].wait_recv()
            block = cols.at[behind[o] * 2 + (core + e) % 2, mine]
            for f, m in enumerate(mates):
                c = remote(block, block, gf_s.at[o, e, f], gf_r.at[o, e, f], m, dp)
                c.start()
                passed.append(c)
    for o in range(1, chips):
        for i in range(2):
            hops[o, i].wait_recv()
            block = h.at[behind[o] * 2 + core, pl.ds(i * half, half)]
            c = remote(block, block, hf_s.at[o, i], hf_r.at[o, i], pipe, sib)
            c.start()
            passed.append(c)
    for c in local:
        c.wait()
    for c in list(cross.values()) + list(hops.values()):
        c.wait_send()
    for c in side + passed:
        c.wait()


def gather(n_pipe, n_dp, g, hid, share):
    rows, ff = hid.shape
    width = g.shape[1] // n_dp
    chips = n_dp // 2
    anywhere = pl.BlockSpec(memory_space=pl.ANY)
    dma = pltpu.SemaphoreType.DMA
    mates = max(share - 1, 1)
    outs = pl.pallas_call(
        functools.partial(gather_kernel, n_dp, share),
        out_shape=[jax.ShapeDtypeStruct((n_dp, rows, w), bf16) for w in (width, ff)],
        in_specs=[anywhere] * 2,
        out_specs=[anywhere] * 2,
        scratch_shapes=[
            dma((2,)), dma((2,)), dma((2,)),
            dma((chips, 2)), dma((chips, 2)),
            dma((chips, 2, mates)), dma((chips, 2, mates)),
            dma((chips, 2)), dma((chips, 2)), dma((chips, 2)), dma((chips, 2)),
        ],
        compiler_params=pltpu.CompilerParams(collective_id=1, has_side_effects=True),
        name="gather_all",
    )(g, hid)
    return [o.reshape(n_dp * rows, o.shape[2]) for o in outs]


def step_kernel(chunk, g_ref, h_ref, w_ref, m_ref, s_ref,
                up_ref, fresh, update_ref, turned, total):
    j = pl.program_id(0)
    ff = h_ref.shape[1]

    @pl.when(j == 0)
    def _():
        total[...] = jnp.zeros_like(total)
        for c in range(0, ff, chunk):
            turned[pl.ds(c, chunk), :] = h_ref[:, pl.ds(c, chunk)].T

    for c in range(0, ff, chunk):
        r = pl.ds(c, chunk)
        grad = jnp.dot(turned[r, :], g_ref[...], preferred_element_type=f32)
        w = w_ref[r, :]
        total[:, r] += lax.dot_general(
            g_ref[...], w.astype(bf16), (((1,), (1,)), ((), ())), preferred_element_type=f32
        )
        top = (beta_one / corr_one) * m_ref[r, :] + ((1.0 - beta_one) / corr_one) * grad
        var = (beta_two / corr_two) * s_ref[r, :] + ((1.0 - beta_two) / corr_two) * (grad * grad)
        update = -(top / (var * lax.rsqrt(var) + epsilon) + decay_rate * w)
        update_ref[r, :] = update
        fresh[r, :] = (w + learn_rate * update).astype(bf16)

    @pl.when(j == pl.num_programs(0) - 1)
    def _():
        up_ref[...] = total[...].astype(bf16)


def step(cols, h, master, moment, second):
    tokens, width = cols.shape
    ff = h.shape[1]
    bn = 512 if width % 512 == 0 else width
    chunk = 256 if ff % 256 == 0 else 128
    whole = pl.BlockSpec((tokens, ff), lambda j: (0, 0), pipeline_mode=pl.Buffered(1))
    tall = pl.BlockSpec((ff, bn), lambda j: (0, j))
    slab = pl.BlockSpec((tokens, bn), lambda j: (0, j))
    return pl.pallas_call(
        functools.partial(step_kernel, chunk),
        grid=(width // bn,),
        out_shape=[
            jax.ShapeDtypeStruct((tokens, ff), bf16),
            jax.ShapeDtypeStruct((ff, width), bf16),
            jax.ShapeDtypeStruct((ff, width), f32),
        ],
        in_specs=[slab, whole, tall, tall, tall],
        out_specs=[pl.BlockSpec((tokens, ff), lambda j: (0, 0)), tall, tall],
        scratch_shapes=[
            pltpu.VMEM((ff, tokens), bf16),
            pltpu.VMEM((tokens, ff), f32),
        ],
        cost_estimate=pl.CostEstimate(
            flops=4 * tokens * ff * width, bytes_accessed=18 * ff * width, transcendentals=ff * width
        ),
        compiler_params=pltpu.CompilerParams(vmem_limit_bytes=56 << 20),
        name="fused_step",
    )(cols, h, master, moment, second)


def reduce_kernel(levels, n_dp, pieces, up_hbm, fresh_hbm, *refs):
    nh_hbm, up_out, next_out = refs[:n_dp], refs[n_dp], refs[n_dp + 1]
    up, nh, fresh, nxt, loc = refs[n_dp + 2:n_dp + 7]
    scratch = refs[n_dp + 7:]
    up_in, up_mid, up_far, us_s, us_r, uf_s, uf_r, n_s, n_r = scratch[:9]
    recv = scratch[9:9 + levels]
    send = (None,) + scratch[9 + levels:8 + 2 * levels]
    keep = (None,) + scratch[8 + 2 * levels:]
    pipe, dp = lax.axis_index("pipe"), lax.axis_index("dp")
    chips = n_dp // 2
    chip, core = dp // 2, dp % 2
    sib = chip * 2 + 1 - core
    ahead = [(chip + o) % chips for o in range(chips)]
    bit = [(pipe // 2**b) % 2 for b in range(levels)]
    across = [pipe + (1 - 2 * bit[b]) * 2**b for b in range(levels)]
    cw = next_out.shape[1] // pieces
    rows = nh_hbm[0].shape[0]
    later = []
    for o in range(n_dp):
        at = pl.multiple_of((dp + n_dp - o) % n_dp * rows, rows)
        later.append(pltpu.make_async_copy(nh_hbm[o], nh.at[pl.ds(at, rows)], loc.at[1 + pieces + o]))
    loads = [pltpu.make_async_copy(up_hbm.at[:, core], up, loc.at[0])]
    loads += [pltpu.make_async_copy(fresh_hbm.at[:, pl.ds(k * cw, cw)],
                                    fresh.at[:, pl.ds(k * cw, cw)], loc.at[1 + k])
              for k in range(pieces)]
    for c in later + loads[1:] + loads[:1]:
        c.start()
    greet([(pipe, sib)] + [(pipe, ahead[o] * 2 + core) for o in range(1, chips)]
          + [(across[b], dp) for b in range(levels)])

    orders = []
    for k in range(pieces):
        order = list(range(levels))
        if k % 2 and levels > 1:
            order[0], order[1] = order[1], order[0]
        orders.append(order)

    def pick(k, j, value):
        left = sorted(orders[k][j:], reverse=True)
        at = left.index(orders[k][j])
        return (ALL,) * at + (value,) + (ALL,) * (len(left) - 1 - at)

    def spot(j, k):
        return (ALL,) * (levels - 1 - j) + (ALL, pl.ds(k * cw, cw))

    flights = {}

    def launch(j, k, src):
        b = orders[k][j]
        flights[j, k] = remote(src, recv[j].at[spot(j, k)], n_s.at[j, k], n_r.at[j, k], across[b], dp)
        flights[j, k].start()

    half = nh.shape[0] // 2
    tail = lambda k: (ALL, pl.ds(k * cw, cw))
    near = {}
    for o in list(range(1, chips)) + [0]:
        near[o] = remote(up_hbm.at[ahead[o], 1 - core], up_in.at[o], us_s.at[o], us_r.at[o], pipe, sib)
        near[o].start()
    for c in later:
        c.wait()
    for k in range(pieces):
        loads[1 + k].wait()
        for t in range(2):
            product = jnp.dot(nh[pl.ds(t * half, half), :], fresh[:, pl.ds(k * cw, cw)],
                              preferred_element_type=f32).astype(bf16)
            nxt[(t,) + (ALL,) * levels + (pl.ds(k * cw, cw),)] = product.reshape(
                (2,) * (levels - 1) + (half // 2 ** (levels - 1), cw))
        launch(0, k, nxt.at[pick(k, 0, 1 - bit[orders[k][0]]) + tail(k)])
    loads[0].wait()
    far = {}
    for o in range(1, chips):
        near[o].wait_recv()
        up_mid[o] = (up[ahead[o]].astype(f32) + up_in[o].astype(f32)).astype(bf16)
        far[o] = remote(up_mid.at[o], up_far.at[o], uf_s.at[o], uf_r.at[o], pipe, ahead[o] * 2 + core)
        far[o].start()

    for j in range(levels):
        for k in range(pieces):
            flights[j, k].wait_recv()

            def summed(index):
                if j == 0:
                    mine = pick(k, 0, bit[orders[k][0]])
                    full, i = [], iter(index)
                    for m in mine:
                        full.append(next(i) if isinstance(m, slice) else m)
                    kept = nxt[tuple(full) + tail(k)]
                else:
                    kept = keep[j][index + tail(k)]
                return kept.astype(f32) + recv[j][index + tail(k)].astype(f32)

            if j < levels - 1:
                b = bit[orders[k][j + 1]]
                send[j + 1][spot(j + 1, k)] = summed(pick(k, j + 1, 1 - b)).astype(bf16)
                launch(j + 1, k, send[j + 1].at[spot(j + 1, k)])
                keep[j + 1][spot(j + 1, k)] = summed(pick(k, j + 1, b))
            else:
                next_out[tail(k)] = summed(()).astype(bf16)

    near[0].wait_recv()
    total = up[chip].astype(f32) + up_in[0].astype(f32)
    for o in range(1, chips):
        far[o].wait_recv()
        total = total + up_far[o].astype(f32)
    up_out[...] = total.astype(bf16)
    for c in list(near.values()) + list(far.values()) + list(flights.values()):
        c.wait_send()


def reduce(n_pipe, n_dp, up, nh, fresh):
    levels = int(math.log2(n_pipe))
    tokens, ff = up.shape
    width = fresh.shape[1]
    rows, few = tokens // n_dp, tokens // n_pipe
    chips = n_dp // 2
    pieces = 8 if width % 2048 == 0 else 4 if width % 512 == 0 else 1
    dma = pltpu.SemaphoreType.DMA
    vmem = pl.BlockSpec(memory_space=pltpu.VMEM)
    hbm = pl.BlockSpec(memory_space=pltpu.HBM)
    shape = lambda j: (2,) * (levels - 1 - j) + (few, width)
    return pl.pallas_call(
        functools.partial(reduce_kernel, levels, n_dp, pieces),
        out_shape=[
            jax.ShapeDtypeStruct((rows, ff), bf16),
            jax.ShapeDtypeStruct((few, width), bf16),
        ],
        in_specs=[hbm] * (2 + n_dp),
        out_specs=[vmem] * 2,
        scratch_shapes=[
            pltpu.VMEM((chips, rows, ff), bf16),
            pltpu.VMEM((tokens, ff), bf16),
            pltpu.VMEM((ff, width), bf16),
            pltpu.VMEM((2,) * levels + (few, width), bf16),
            dma((1 + pieces + n_dp,)),
        ]
        + [pltpu.VMEM((chips, rows, ff), bf16)] * 3
        + [dma((chips,))] * 4
        + [dma((levels, pieces))] * 2
        + [pltpu.VMEM(shape(j), bf16) for j in range(levels)]
        + [pltpu.VMEM(shape(j), bf16) for j in range(1, levels)]
        + [pltpu.VMEM(shape(j), f32) for j in range(1, levels)],
        compiler_params=pltpu.CompilerParams(
            collective_id=2, has_side_effects=True, vmem_limit_bytes=62 << 20
        ),
        name="reduce_both",
    )(up.reshape(chips, 2, rows, ff), fresh, *nh)


def on_device(n_pipe, n_dp, grad_output, hidden, next_hidden, master, moment, second_moment):
    share = 4 if n_pipe % 4 == 0 else 1
    cols, h = gather(n_pipe, n_dp, grad_output, hidden, share)
    later, cols = lax.optimization_barrier((next_hidden, cols))
    nh = [later] + [
        lax.ppermute(later, "dp", [(i, (i + o) % n_dp) for i in range(n_dp)]) for o in range(1, n_dp)
    ]
    up, fresh, update = step(cols, h, master, moment, second_moment)
    upstream, next_out = reduce(n_pipe, n_dp, up, nh, fresh)
    return (update, upstream, next_out)


def solution(mesh):
    in_specs = (
        P("dp", None),
        P("dp", "pipe"),
        P("dp", "pipe"),
        P("pipe", "dp"),
        P("pipe", "dp"),
        P("pipe", "dp"),
    )
    out_specs = (P("pipe", "dp"), P("dp", "pipe"), P("pipe", "dp"))
    return jax.shard_map(
        functools.partial(on_device, mesh.shape["pipe"], mesh.shape["dp"]),
        mesh=mesh, in_specs=in_specs, out_specs=out_specs, check_vma=False,
    )
```

```python
import functools
import math

import jax
import jax.numpy as jnp
from jax import lax
from jax.experimental import pallas as pl
from jax.experimental.pallas import tpu as pltpu
from jax.sharding import PartitionSpec as P

beta_one = 0.9
beta_two = 0.95
corr_one = 1.0 - 0.9**10
corr_two = 1.0 - 0.95**10
learn_rate = 0.005
decay_rate = 0.1
epsilon = 1e-08

f32 = jnp.float32
bf16 = jnp.bfloat16
MESH = pl.DeviceIdType.MESH
ALL = slice(None)


def remote(src, dst, send, recv, pipe, dp):
    return pltpu.make_async_remote_copy(
        src_ref=src, dst_ref=dst, send_sem=send, recv_sem=recv,
        device_id=(pipe, dp), device_id_type=MESH,
    )


def greet(partners):
    barrier = pltpu.get_barrier_semaphore()
    for partner in partners:
        pl.semaphore_signal(barrier, inc=1, device_id=partner, device_id_type=MESH)
    pl.semaphore_wait(barrier, len(partners))


def gather_kernel(n_dp, share, g, hid, cols, h, loc, sib_s, sib_r,
                  g_s, g_r, gf_s, gf_r, h_s, h_r, hf_s, hf_r):
    pipe, dp = lax.axis_index("pipe"), lax.axis_index("dp")
    chips = n_dp // 2
    chip, core = dp // 2, dp % 2
    sib = chip * 2 + 1 - core
    rows, width = cols.shape[1], cols.shape[2]
    part = rows // share
    q = pipe % share
    base = pipe - q
    mine = pl.ds(pl.multiple_of(q * part, part), part)

    def columns(d):
        return pl.ds(pl.multiple_of(d * width, width), width)

    mates = [base + (q + f) % share for f in range(1, share)]
    ahead = [(chip + o) % chips for o in range(chips)]
    behind = [(chip + chips - o) % chips for o in range(chips)]
    partners = [(pipe, sib)]
    partners += [(pipe, ahead[o] * 2 + (core + e) % 2) for o in range(1, chips) for e in range(2)]
    partners += [(m, dp) for m in mates]

    local = [
        pltpu.make_async_copy(g.at[:, columns(dp)], cols.at[dp], loc.at[0]),
        pltpu.make_async_copy(hid, h.at[dp], loc.at[1]),
    ]
    for c in local:
        c.start()
    greet(partners)

    cross = {}
    for o in range(1, chips):
        for e in range(2):
            d = ahead[o] * 2 + (core + e) % 2
            cross[o, e] = remote(g.at[mine, columns(d)], cols.at[dp, mine],
                                 g_s.at[o, e], g_r.at[o, e], pipe, d)
            cross[o, e].start()
    half = rows // 2
    hops = {}
    for o in range(1, chips):
        for i in range(2):
            some = pl.ds(i * half, half)
            hops[o, i] = remote(hid.at[some], h.at[dp, some], h_s.at[o, i], h_r.at[o, i],
                                pipe, ahead[o] * 2 + core)
            hops[o, i].start()
    side = [
        remote(g.at[:, columns(sib)], cols.at[dp], sib_s.at[0], sib_r.at[0], pipe, sib),
        remote(hid, h.at[dp], sib_s.at[1], sib_r.at[1], pipe, sib),
    ]
    for c in side:
        c.start()
    passed = []
    for o in range(1, chips):
        for e in range(2):
            cross[o, e].wait_recv()
            block = cols.at[behind[o] * 2 + (core + e) % 2, mine]
            for f, m in enumerate(mates):
                c = remote(block, block, gf_s.at[o, e, f], gf_r.at[o, e, f], m, dp)
                c.start()
                passed.append(c)
    for o in range(1, chips):
        for i in range(2):
            hops[o, i].wait_recv()
            block = h.at[behind[o] * 2 + core, pl.ds(i * half, half)]
            c = remote(block, block, hf_s.at[o, i], hf_r.at[o, i], pipe, sib)
            c.start()
            passed.append(c)
    for c in local:
        c.wait()
    for c in list(cross.values()) + list(hops.values()):
        c.wait_send()
    for c in side + passed:
        c.wait()


def gather(n_pipe, n_dp, g, hid, share):
    rows, ff = hid.shape
    width = g.shape[1] // n_dp
    chips = n_dp // 2
    anywhere = pl.BlockSpec(memory_space=pl.ANY)
    dma = pltpu.SemaphoreType.DMA
    mates = max(share - 1, 1)
    outs = pl.pallas_call(
        functools.partial(gather_kernel, n_dp, share),
        out_shape=[jax.ShapeDtypeStruct((n_dp, rows, w), bf16) for w in (width, ff)],
        in_specs=[anywhere] * 2,
        out_specs=[anywhere] * 2,
        scratch_shapes=[
            dma((2,)), dma((2,)), dma((2,)),
            dma((chips, 2)), dma((chips, 2)),
            dma((chips, 2, mates)), dma((chips, 2, mates)),
            dma((chips, 2)), dma((chips, 2)), dma((chips, 2)), dma((chips, 2)),
        ],
        compiler_params=pltpu.CompilerParams(collective_id=1, has_side_effects=True),
        name="gather_all",
    )(g, hid)
    return [o.reshape(n_dp * rows, o.shape[2]) for o in outs]


def step_kernel(chunk, g_ref, h_ref, w_ref, m_ref, s_ref,
                up_ref, fresh, update_ref, turned, total):
    j = pl.program_id(0)
    ff = h_ref.shape[1]

    @pl.when(j == 0)
    def _():
        total[...] = jnp.zeros_like(total)
        for c in range(0, ff, chunk):
            turned[pl.ds(c, chunk), :] = h_ref[:, pl.ds(c, chunk)].T

    for c in range(0, ff, chunk):
        r = pl.ds(c, chunk)
        grad = jnp.dot(turned[r, :], g_ref[...], preferred_element_type=f32)
        w = w_ref[r, :]
        total[:, r] += lax.dot_general(
            g_ref[...], w.astype(bf16), (((1,), (1,)), ((), ())), preferred_element_type=f32
        )
        top = (beta_one / corr_one) * m_ref[r, :] + ((1.0 - beta_one) / corr_one) * grad
        var = (beta_two / corr_two) * s_ref[r, :] + ((1.0 - beta_two) / corr_two) * (grad * grad)
        update = -(top / (var * lax.rsqrt(var) + epsilon) + decay_rate * w)
        update_ref[r, :] = update
        fresh[r, :] = (w + learn_rate * update).astype(bf16)

    @pl.when(j == pl.num_programs(0) - 1)
    def _():
        up_ref[...] = total[...].astype(bf16)


def step(cols, h, master, moment, second):
    tokens, width = cols.shape
    ff = h.shape[1]
    bn = 512 if width % 512 == 0 else width
    chunk = 256 if ff % 256 == 0 else 128
    whole = pl.BlockSpec((tokens, ff), lambda j: (0, 0), pipeline_mode=pl.Buffered(1))
    tall = pl.BlockSpec((ff, bn), lambda j: (0, j))
    slab = pl.BlockSpec((tokens, bn), lambda j: (0, j))
    return pl.pallas_call(
        functools.partial(step_kernel, chunk),
        grid=(width // bn,),
        out_shape=[
            jax.ShapeDtypeStruct((tokens, ff), bf16),
            jax.ShapeDtypeStruct((ff, width), bf16),
            jax.ShapeDtypeStruct((ff, width), f32),
        ],
        in_specs=[slab, whole, tall, tall, tall],
        out_specs=[pl.BlockSpec((tokens, ff), lambda j: (0, 0)), tall, tall],
        scratch_shapes=[
            pltpu.VMEM((ff, tokens), bf16),
            pltpu.VMEM((tokens, ff), f32),
        ],
        cost_estimate=pl.CostEstimate(
            flops=4 * tokens * ff * width, bytes_accessed=18 * ff * width, transcendentals=ff * width
        ),
        compiler_params=pltpu.CompilerParams(vmem_limit_bytes=56 << 20),
        name="fused_step",
    )(cols, h, master, moment, second)


def reduce_kernel(levels, n_dp, pieces, up_hbm, fresh_hbm, *refs):
    nh_hbm, up_out, next_out = refs[:n_dp], refs[n_dp], refs[n_dp + 1]
    up, nh, fresh, nxt, loc = refs[n_dp + 2:n_dp + 7]
    scratch = refs[n_dp + 7:]
    up_in, up_mid, up_far, us_s, us_r, uf_s, uf_r, n_s, n_r = scratch[:9]
    recv = scratch[9:9 + levels]
    send = (None,) + scratch[9 + levels:8 + 2 * levels]
    keep = (None,) + scratch[8 + 2 * levels:]
    pipe, dp = lax.axis_index("pipe"), lax.axis_index("dp")
    chips = n_dp // 2
    chip, core = dp // 2, dp % 2
    sib = chip * 2 + 1 - core
    ahead = [(chip + o) % chips for o in range(chips)]
    bit = [(pipe // 2**b) % 2 for b in range(levels)]
    across = [pipe + (1 - 2 * bit[b]) * 2**b for b in range(levels)]
    cw = next_out.shape[1] // pieces
    rows = nh_hbm[0].shape[0]
    later = []
    for o in range(n_dp):
        at = pl.multiple_of((dp + n_dp - o) % n_dp * rows, rows)
        later.append(pltpu.make_async_copy(nh_hbm[o], nh.at[pl.ds(at, rows)], loc.at[1 + pieces + o]))
    loads = [pltpu.make_async_copy(up_hbm.at[:, core], up, loc.at[0])]
    loads += [pltpu.make_async_copy(fresh_hbm.at[:, pl.ds(k * cw, cw)],
                                    fresh.at[:, pl.ds(k * cw, cw)], loc.at[1 + k])
              for k in range(pieces)]
    for c in later + loads[1:] + loads[:1]:
        c.start()
    greet([(pipe, sib)] + [(pipe, ahead[o] * 2 + core) for o in range(1, chips)]
          + [(across[b], dp) for b in range(levels)])

    orders = []
    for k in range(pieces):
        order = list(range(levels))
        if k % 2 and levels > 1:
            order[0], order[1] = order[1], order[0]
        orders.append(order)

    def pick(k, j, value):
        left = sorted(orders[k][j:], reverse=True)
        at = left.index(orders[k][j])
        return (ALL,) * at + (value,) + (ALL,) * (len(left) - 1 - at)

    def spot(j, k):
        return (ALL,) * (levels - 1 - j) + (ALL, pl.ds(k * cw, cw))

    flights = {}

    def launch(j, k, src):
        b = orders[k][j]
        flights[j, k] = remote(src, recv[j].at[spot(j, k)], n_s.at[j, k], n_r.at[j, k], across[b], dp)
        flights[j, k].start()

    half = nh.shape[0] // 2
    tail = lambda k: (ALL, pl.ds(k * cw, cw))
    near = {}
    for o in list(range(1, chips)) + [0]:
        near[o] = remote(up_hbm.at[ahead[o], 1 - core], up_in.at[o], us_s.at[o], us_r.at[o], pipe, sib)
        near[o].start()
    for c in later:
        c.wait()
    for k in range(pieces):
        loads[1 + k].wait()
        for t in range(2):
            product = jnp.dot(nh[pl.ds(t * half, half), :], fresh[:, pl.ds(k * cw, cw)],
                              preferred_element_type=f32).astype(bf16)
            nxt[(t,) + (ALL,) * levels + (pl.ds(k * cw, cw),)] = product.reshape(
                (2,) * (levels - 1) + (half // 2 ** (levels - 1), cw))
        launch(0, k, nxt.at[pick(k, 0, 1 - bit[orders[k][0]]) + tail(k)])
    loads[0].wait()
    far = {}
    for o in range(1, chips):
        near[o].wait_recv()
        up_mid[o] = (up[ahead[o]].astype(f32) + up_in[o].astype(f32)).astype(bf16)
        far[o] = remote(up_mid.at[o], up_far.at[o], uf_s.at[o], uf_r.at[o], pipe, ahead[o] * 2 + core)
        far[o].start()

    for j in range(levels):
        for k in range(pieces):
            flights[j, k].wait_recv()

            def summed(index):
                if j == 0:
                    mine = pick(k, 0, bit[orders[k][0]])
                    full, i = [], iter(index)
                    for m in mine:
                        full.append(next(i) if isinstance(m, slice) else m)
                    kept = nxt[tuple(full) + tail(k)]
                else:
                    kept = keep[j][index + tail(k)]
                return kept.astype(f32) + recv[j][index + tail(k)].astype(f32)

            if j < levels - 1:
                b = bit[orders[k][j + 1]]
                send[j + 1][spot(j + 1, k)] = summed(pick(k, j + 1, 1 - b)).astype(bf16)
                launch(j + 1, k, send[j + 1].at[spot(j + 1, k)])
                keep[j + 1][spot(j + 1, k)] = summed(pick(k, j + 1, b))
            else:
                next_out[tail(k)] = summed(()).astype(bf16)

    near[0].wait_recv()
    total = up[chip].astype(f32) + up_in[0].astype(f32)
    for o in range(1, chips):
        far[o].wait_recv()
        total = total + up_far[o].astype(f32)
    up_out[...] = total.astype(bf16)
    for c in list(near.values()) + list(far.values()) + list(flights.values()):
        c.wait_send()


def reduce(n_pipe, n_dp, up, nh, fresh):
    levels = int(math.log2(n_pipe))
    tokens, ff = up.shape
    width = fresh.shape[1]
    rows, few = tokens // n_dp, tokens // n_pipe
    chips = n_dp // 2
    pieces = 8 if width % 2048 == 0 else 4 if width % 512 == 0 else 1
    dma = pltpu.SemaphoreType.DMA
    vmem = pl.BlockSpec(memory_space=pltpu.VMEM)
    hbm = pl.BlockSpec(memory_space=pltpu.HBM)
    shape = lambda j: (2,) * (levels - 1 - j) + (few, width)
    return pl.pallas_call(
        functools.partial(reduce_kernel, levels, n_dp, pieces),
        out_shape=[
            jax.ShapeDtypeStruct((rows, ff), bf16),
            jax.ShapeDtypeStruct((few, width), bf16),
        ],
        in_specs=[hbm] * (2 + n_dp),
        out_specs=[vmem] * 2,
        scratch_shapes=[
            pltpu.VMEM((chips, rows, ff), bf16),
            pltpu.VMEM((tokens, ff), bf16),
            pltpu.VMEM((ff, width), bf16),
            pltpu.VMEM((2,) * levels + (few, width), bf16),
            dma((1 + pieces + n_dp,)),
        ]
        + [pltpu.VMEM((chips, rows, ff), bf16)] * 3
        + [dma((chips,))] * 4
        + [dma((levels, pieces))] * 2
        + [pltpu.VMEM(shape(j), bf16) for j in range(levels)]
        + [pltpu.VMEM(shape(j), bf16) for j in range(1, levels)]
        + [pltpu.VMEM(shape(j), f32) for j in range(1, levels)],
        compiler_params=pltpu.CompilerParams(
            collective_id=2, has_side_effects=True, vmem_limit_bytes=60 << 20
        ),
        name="reduce_both",
    )(up.reshape(chips, 2, rows, ff), fresh, *nh)


def on_device(n_pipe, n_dp, grad_output, hidden, next_hidden, master, moment, second_moment):
    share = 4 if n_pipe % 4 == 0 else 1
    cols, h = gather(n_pipe, n_dp, grad_output, hidden, share)
    later, cols = lax.optimization_barrier((next_hidden, cols))
    nh = [later] + [
        lax.ppermute(later, "dp", [(i, (i + o) % n_dp) for i in range(n_dp)]) for o in range(1, n_dp)
    ]
    up, fresh, update = step(cols, h, master, moment, second_moment)
    upstream, next_out = reduce(n_pipe, n_dp, up, nh, fresh)
    return (update, upstream, next_out)


def solution(mesh):
    in_specs = (
        P("dp", None),
        P("dp", "pipe"),
        P("dp", "pipe"),
        P("pipe", "dp"),
        P("pipe", "dp"),
        P("pipe", "dp"),
    )
    out_specs = (P("pipe", "dp"), P("dp", "pipe"), P("pipe", "dp"))
    return jax.shard_map(
        functools.partial(on_device, mesh.shape["pipe"], mesh.shape["dp"]),
        mesh=mesh, in_specs=in_specs, out_specs=out_specs, check_vma=False,
    )
```
